32 devices in a mesh: groups: 2 (over y), freq: 16 (over z, x, core).
Axes of the slice: x: 2, y: 2, z: 4, core: 2. Of those that a mesh axis runs over, the one named last changes fastest.
Arguments:
- refl: bfloat16 [128, 2, 512, 512], P(('groups', 'freq')), parts along dimension 0, may hold values from -0.1875 to 0.1875
- refl_scale: float32 [128, 4], P(('groups', 'freq')), parts along dimension 0, may hold values from 0.5 to 4
- freq_index: int32 [128], P(('groups', 'freq')), parts along dimension 0, may hold values from 1 to 1023, as said below
- fd_plus: bfloat16 [4096, 32, 512], P(('groups', 'freq')), parts along dimension 0, may hold values from -6 to 6
- onset: int32 [32768], P(('groups', 'freq')), parts along dimension 0, may hold values from 128 to 767
Outputs:
- f_minus: bfloat16 [4096, 32, 512], P(('groups', 'freq')), parts along dimension 0
- f_plus: float32 [4096, 32, 512], P(('groups', 'freq')), parts along dimension 0
The draws below stay inside these ranges and needn't reach their ends.
There are 2 independent parts, one for each index of `groups`. The reference program is written for one: setup_inputs(seed, part) draws one part's arguments, and reference() takes and returns one part's arrays. A program takes and returns all parts, laid end to end along the dimension named above; each array names one. Nothing has to cross between parts.
Inputs may be any that keep to these rules, and one draw needn't show every extreme that they name: `freq_index`: the bins are distinct and ascending; the first is 1 and the last is 1023.
All inputs are finite; a program needn't handle non-finite values.
Results may differ from the reference program's by a relative error of at most 0.01.
Values may be sent and summed in bfloat16 or wider, within the bound.
No kernel may reach another device: no remote copies, remote signals or barrier semaphores. Data moves between devices by JAX's collectives and lax.ppermute only.
A program may use at most 128 MiB of HBM per device.

```python
import math
import jax
import jax.numpy as jnp
from jax import lax

NT = 2048
VP = 32
NREC = 512
NF = 64
COLS = 16384


def draw_freq_index(key, part):
    inner = jax.random.permutation(key, NT // 2 - 3).astype(jnp.int32) + 2
    chosen = inner[:NF - 2]
    ends = jnp.array([1, NT // 2 - 1], dtype=jnp.int32)
    return jnp.sort(jnp.concatenate([ends, chosen]))


def touch_ends(entries, stream_key, least, top_value):
    dims = entries.shape
    spot = [jax.random.randint(jax.random.fold_in(stream_key, axis), (), 0, dims[axis]) for axis in range(len(dims))]
    entries = entries.at[tuple(spot)].set(least)
    longest = dims.index(max(dims))
    spot[longest] = (spot[longest] + 1) % dims[longest]
    return entries.at[tuple(spot)].set(top_value)


def steps_of(rng, dims, cuts, smallest, high):
    loudness = 1.0
    for axis_at, blocks in cuts:
        heights = jax.random.uniform(jax.random.fold_in(jax.random.fold_in(rng, 6), axis_at), (blocks,), jnp.float32, smallest / len(cuts), high / len(cuts))
        loudness = loudness * jnp.repeat(jnp.exp(heights), dims[axis_at] // blocks).reshape((-1,) + (1,) * (len(dims) - 1 - axis_at))
    return loudness


def normal_values(rng, shape, deviation, most, pieces=(), kind=jnp.bfloat16):
    result = jax.random.normal(rng, shape, jnp.float32) * deviation
    if len(pieces) > 0:
        result = steps_of(rng, shape, pieces, -0.22, 0.18) * result
    return jnp.clip(result, min=-most, max=most).astype(kind)


def setup_inputs(seed: int = 0, part: int = 0) -> dict:
    key_list = jax.random.split(jax.random.key(seed), 6)
    part_splits = jax.random.split(jax.random.fold_in(key_list[5], part), 6)
    return {
        "refl": normal_values(part_splits[0], (NF, 2, NREC, NREC), (2 * NREC) ** -0.5, 0.1875, ((0, 16),)),
        "refl_scale": jnp.clip(jnp.exp(math.log(4.0) - 2.0794415 * jax.random.uniform(part_splits[1], (NF, NREC // 128), jnp.float32) ** steps_of(part_splits[1], (NF, NREC // 128), ((0, 16),), -0.2, 0.2)), 0.5, 4.0),
        "freq_index": draw_freq_index(jax.random.fold_in(jax.random.fold_in(key_list[5], part), 71), part),
        "fd_plus": normal_values(part_splits[3], (NT, VP, NREC), 1.0, 6.0, ((0, 16),)),
        "onset": touch_ends(jax.random.randint(part_splits[4], (COLS,), NT // 16, 3 * NT // 8), jax.random.fold_in(part_splits[4], 1), NT // 16, (3 * NT // 8) - 1).astype(jnp.int32),
    }


def tables(freq_index):
    times = jnp.arange(NT, dtype=jnp.int32)
    phase = (freq_index.astype(jnp.int32)[:, None] * times[None, :]) % NT
    angle = phase.astype(jnp.float32) * jnp.float32(2.0 * math.pi / NT)
    cosine = jnp.cos(angle).astype(jnp.bfloat16).astype(jnp.float32)
    sine = jnp.sin(angle).astype(jnp.bfloat16).astype(jnp.float32)
    return cosine, sine


def forward(field, cosine, sine, colscale):
    data = field.astype(jnp.float32)
    real = jnp.dot(cosine, data, precision=lax.Precision.HIGHEST, preferred_element_type=jnp.float32)
    imag = -jnp.dot(sine, data, precision=lax.Precision.HIGHEST, preferred_element_type=jnp.float32)
    return (real * colscale).astype(jnp.bfloat16), (imag * colscale).astype(jnp.bfloat16)


def convolve(refl, spec_r, spec_i, sign):
    spec_r = spec_r.reshape(NF, VP, NREC)
    spec_i = spec_i.reshape(NF, VP, NREC)

    def one_freq(item):
        resp, xr, xi = item
        resp_r = resp[0].astype(jnp.float32)
        resp_i = resp[1].astype(jnp.float32)
        xr = xr.astype(jnp.float32)
        xi = xi.astype(jnp.float32)
        hp = lax.Precision.HIGHEST
        out_r = jnp.dot(xr, resp_r.T, precision=hp) - sign * jnp.dot(xi, resp_i.T, precision=hp)
        out_i = jnp.dot(xi, resp_r.T, precision=hp) + sign * jnp.dot(xr, resp_i.T, precision=hp)
        return out_r.astype(jnp.bfloat16), out_i.astype(jnp.bfloat16)

    out_r, out_i = lax.map(one_freq, (refl, spec_r, spec_i))
    return out_r.reshape(NF, COLS), out_i.reshape(NF, COLS)


def inverse(out_r, out_i, cosine, sine, keep):
    hp = lax.Precision.HIGHEST
    trace = jnp.dot(cosine.T, out_r.astype(jnp.float32), precision=hp) - jnp.dot(sine.T, out_i.astype(jnp.float32), precision=hp)
    return (trace * jnp.float32(2.0 / NT) * keep).astype(jnp.bfloat16)


def reference(refl, refl_scale, freq_index, fd_plus, onset):
    cosine, sine = tables(freq_index)
    nblocks = refl_scale.shape[1]
    source = jnp.arange(COLS, dtype=jnp.int32) % NREC
    colscale = refl_scale[:, source // (NREC // nblocks)].astype(jnp.float32)
    times = jnp.arange(NT, dtype=jnp.int32)
    signed = jnp.where(times < NT // 2, times, times - NT)
    keep = (jnp.abs(signed)[:, None] < onset[None, :]).astype(jnp.float32)
    direct = fd_plus.reshape(NT, COLS)
    spec_r, spec_i = forward(direct, cosine, sine, colscale)
    out_r, out_i = convolve(refl, spec_r, spec_i, 1.0)
    minus = inverse(out_r, out_i, cosine, sine, keep)
    spec_r, spec_i = forward(minus, cosine, sine, colscale)
    out_r, out_i = convolve(refl, spec_r, spec_i, -1.0)
    update = inverse(out_r, out_i, cosine, sine, keep)
    plus = direct.astype(jnp.float32) + update.astype(jnp.float32)
    return minus.reshape(NT, VP, NREC), plus.reshape(NT, VP, NREC)
```

```python
import functools
import math

import jax
import jax.numpy as jnp
from jax import lax
from jax.experimental import pallas as pl
from jax.experimental.pallas import tpu as pltpu
from jax.sharding import PartitionSpec as P

ONSET_TOP = 767
VMEM_LIMIT = 56 << 20


def params():
    return pltpu.CompilerParams(vmem_limit_bytes=VMEM_LIMIT)


def swap(x, stride):
    n = lax.axis_size("freq")
    return lax.ppermute(x, "freq", [(i, i ^ stride) for i in range(n)])


def cos_table(bins, rows_quarter, times, ntime):
    phase = (bins * times + rows_quarter) % ntime
    angle = phase.astype(jnp.float32) * jnp.float32(2.0 * math.pi / ntime)
    return jnp.cos(angle)


def points_major(x):
    t, v, s = x.shape
    sb = 128

    def kernel(x_ref, o_ref, scr):
        scr[...] = x_ref[...].astype(jnp.float32).reshape(t * v, sb)
        for i in range(v):
            o_ref[i] = scr[pl.ds(i, t, stride=v), :].astype(jnp.bfloat16)

    return pl.pallas_call(
        kernel,
        grid=(s // sb,),
        in_specs=[pl.BlockSpec((t, v, sb), lambda i: (0, 0, i))],
        out_specs=pl.BlockSpec((v, t, sb), lambda i: (0, 0, i)),
        out_shape=jax.ShapeDtypeStruct((v, t, s), x.dtype),
        scratch_shapes=[pltpu.VMEM((t * v, sb), jnp.float32)],
        compiler_params=params(),
        name="points_major",
    )(x)


def partial_spectra(table, own, other, rb, nq):
    rows, _ = table.shape
    v, t, s = own.shape
    ndest = rows // rb
    c = s // nq
    vb = 4 if v % 4 == 0 else 1

    def kernel(tab_ref, own_ref, other_ref, *outs):
        for i in range(vb):
            x = jnp.concatenate([own_ref[i], other_ref[i]], axis=0)
            res = jnp.dot(tab_ref[...], x, preferred_element_type=jnp.float32)
            for j in range(ndest):
                part = res[j * rb : (j + 1) * rb].astype(jnp.bfloat16)
                for q in range(nq):
                    outs[j][i, q] = part[:, q * c : (q + 1) * c]

    return pl.pallas_call(
        kernel,
        grid=(v // vb,),
        in_specs=[
            pl.BlockSpec((rows, 2 * t), lambda i: (0, 0)),
            pl.BlockSpec((vb, t, s), lambda i: (i, 0, 0)),
            pl.BlockSpec((vb, t, s), lambda i: (i, 0, 0)),
        ],
        out_specs=[pl.BlockSpec((vb, nq, rb, c), lambda i: (i, 0, 0, 0))] * ndest,
        out_shape=[jax.ShapeDtypeStruct((v, nq, rb, c), jnp.bfloat16)] * ndest,
        compiler_params=params(),
        name="partial_spectra",
    )(table, own, other)


def convolve(parts, scale, refl, sign):
    v, nq, rb, c = parts[0].shape
    nf, _, r, s = refl.shape
    nparts = len(parts)

    def kernel(*refs):
        part_refs = refs[:nparts]
        scale_ref = None if scale is None else refs[nparts]
        refl_ref, out_ref, x_scr, y_scr = refs[-4:]
        k = pl.program_id(0)

        @pl.when(k == 0)
        def _():
            for i in range(v):
                for q in range(nq):
                    x = part_refs[0][i, q].astype(jnp.float32)
                    for ref in part_refs[1:]:
                        x = x + ref[i, q].astype(jnp.float32)
                    if scale_ref is not None:
                        x = x * scale_ref[:, q * c : (q + 1) * c]
                    for b in range(c // 128):
                        x_scr[q * (c // 128) + b, pl.ds(i, rb, stride=v), :] = x[
                            :, b * 128 : (b + 1) * 128
                        ]

        rows = pl.ds(pl.multiple_of(k * 2 * v, 2 * v), 2 * v)
        x = jnp.concatenate(
            [x_scr[b, rows, :].astype(jnp.bfloat16) for b in range(s // 128)], axis=1
        )
        dims = (((1,), (1,)), ((), ()))
        a = lax.dot_general(x, refl_ref[0, 0], dims, preferred_element_type=jnp.float32)
        b = lax.dot_general(x, refl_ref[0, 1], dims, preferred_element_type=jnp.float32)
        y = jnp.concatenate([a[:v] - sign * b[v:], a[v:] + sign * b[:v]], axis=0)
        for b in range(r // 128):
            y_scr[b, rows, :] = y[:, b * 128 : (b + 1) * 128]

        @pl.when(k == nf - 1)
        def _():
            for i in range(v):
                for q in range(nq):
                    for b in range(c // 128):
                        y = y_scr[q * (c // 128) + b, pl.ds(i, rb, stride=v), :]
                        out_ref[i, q, :, b * 128 : (b + 1) * 128] = y.astype(jnp.bfloat16)

    whole = pl.BlockSpec((v, nq, rb, c), lambda k: (0, 0, 0, 0))
    args = list(parts)
    specs = [whole] * nparts
    if scale is not None:
        args.append(scale)
        specs.append(pl.BlockSpec((rb, s), lambda k: (0, 0)))
    args.append(refl)
    specs.append(pl.BlockSpec((1, 2, r, s), lambda k: (k, 0, 0, 0)))
    return pl.pallas_call(
        kernel,
        grid=(nf,),
        in_specs=specs,
        out_specs=whole,
        out_shape=jax.ShapeDtypeStruct((v, nq, rb, c), jnp.bfloat16),
        scratch_shapes=[
            pltpu.VMEM((s // 128, rb * v, 128), jnp.float32),
            pltpu.VMEM((r // 128, rb * v, 128), jnp.float32),
        ],
        compiler_params=params(),
        name="convolve",
    )(*args)


def window_columns(y, inv_table, fwd_table, absq, onset, scale):
    n, h, rb, c = y.shape
    rows = n * rb
    th = inv_table.shape[0]
    tb = 256

    def kernel(y_ref, inv_ref, fwd_ref, q_ref, onset_ref, scale_ref, out_ref):
        for i in range(h):
            spec = jnp.concatenate([y_ref[j, i] for j in range(n)], axis=0)
            acc = jnp.zeros((rows, c), jnp.float32)
            for k in range(th // tb):
                at = slice(k * tb, (k + 1) * tb)
                trace = jnp.dot(inv_ref[at, :], spec, preferred_element_type=jnp.float32)
                kept = q_ref[at, :] < onset_ref[i]
                trace = jnp.where(kept, trace, 0.0).astype(jnp.bfloat16)
                acc += jnp.dot(fwd_ref[:, at], trace, preferred_element_type=jnp.float32)
            acc = (acc * scale_ref[:, i * c : (i + 1) * c]).astype(jnp.bfloat16)
            for j in range(n):
                out_ref[j, i] = acc[j * rb : (j + 1) * rb]

    return pl.pallas_call(
        kernel,
        out_shape=jax.ShapeDtypeStruct((n, h, rb, c), jnp.bfloat16),
        compiler_params=params(),
        name="window_columns",
    )(y, inv_table, fwd_table, absq, onset, scale)


def time_block(pieces, table, absq, onset, direct, t):
    v, nq, rb, c = pieces[0].shape
    npieces = len(pieces)
    s = nq * c
    sb = 128
    vb = 2 if v % 2 == 0 else 1
    tb = 8

    def kernel(*refs):
        piece_refs = refs[:npieces]
        tab_ref, q_ref, onset_ref = refs[npieces : npieces + 3]
        direct_ref = None if direct is None else refs[npieces + 3]
        out_ref, scr = refs[-2:]
        for i in range(0, v, vb):
            spec = jnp.concatenate(
                [
                    jnp.concatenate([ref[i + j, 0] for ref in piece_refs], axis=0)
                    for j in range(vb)
                ],
                axis=1,
            )
            res = jnp.dot(tab_ref[...], spec, preferred_element_type=jnp.float32)
            for j in range(vb):
                kept = q_ref[...] < onset_ref[i + j : i + j + 1, :]
                y = jnp.where(kept, res[:, j * sb : (j + 1) * sb], 0.0)
                scr[pl.ds(i + j, t, stride=v), :] = y

        @pl.loop(0, t // tb)
        def _(k):
            y = scr[pl.ds(pl.multiple_of(k * tb * v, tb * v), tb * v), :]
            y = y.astype(jnp.bfloat16).reshape(tb, v, sb)
            at = pl.ds(k * tb, tb)
            if direct_ref is None:
                out_ref[at] = y
            else:
                out_ref[at] = direct_ref[at].astype(jnp.float32) + y.astype(jnp.float32)

    per = c // sb
    piece_spec = pl.BlockSpec((v, 1, rb, sb), lambda i: (0, i // per, 0, i % per))
    field_spec = pl.BlockSpec((t, v, sb), lambda i: (0, 0, i))
    args = list(pieces) + [table, absq, onset]
    specs = [piece_spec] * npieces + [
        pl.BlockSpec(table.shape, lambda i: (0, 0)),
        pl.BlockSpec(absq.shape, lambda i: (0, 0)),
        pl.BlockSpec((v, sb), lambda i: (0, i)),
    ]
    if direct is not None:
        args.append(direct)
        specs.append(field_spec)
    dtype = jnp.bfloat16 if direct is None else jnp.float32
    return pl.pallas_call(
        kernel,
        grid=(s // sb,),
        in_specs=specs,
        out_specs=field_spec,
        out_shape=jax.ShapeDtypeStruct((t, v, s), dtype),
        scratch_shapes=[pltpu.VMEM((t * v, sb), jnp.float32)],
        compiler_params=params(),
        name="time_block",
    )(*args)


def local(refl, refl_scale, freq_index, fd_plus, onset):
    nf = refl.shape[0]
    nrec = refl.shape[2]
    t, v, _ = fd_plus.shape
    n = lax.axis_size("freq")
    me = lax.axis_index("freq")
    nz = n // 4
    ntime = t * n
    columns = v * nrec
    width = columns // n
    c = min(width, nrec)
    nq = nrec // c
    h = width // c
    rb = 2 * nf
    nblocks = refl_scale.shape[1]
    quarter = ntime // 4

    info = jnp.concatenate(
        [onset.astype(jnp.float32), freq_index.astype(jnp.float32), refl_scale.reshape(-1)]
    )
    pad = -info.shape[0] % 128
    info = jnp.pad(info, (0, pad)).reshape(-1, 128)
    pair = jnp.stack([info, swap(info, 1)])
    quad = jnp.stack([pair, swap(pair, 2)])
    infos = jnp.stack([quad] + [swap(quad, 4 * d) for d in range(1, nz)])
    infos = infos.reshape(n, -1)
    bins_rel = infos[:, width : width + nf].astype(jnp.int32)

    ids = jnp.arange(n, dtype=jnp.int32)
    chosen = (ids[:, None] ^ me) == ids[None, :]
    infos_abs = jnp.sum(jnp.where(chosen[:, :, None], infos[None], 0.0), axis=1)
    onset_all = infos_abs[:, :width].astype(jnp.int32).reshape(v, nrec)
    bins_abs = infos_abs[:, width : width + nf].astype(jnp.int32)
    scale_abs = infos_abs[:, width + nf : width + nf + nf * nblocks].reshape(n * nf, nblocks)

    ri = jnp.arange(2, dtype=jnp.int32) * quarter
    def bin_rows(b):
        return jnp.broadcast_to(b.reshape(-1, 1), (b.size, 2)).reshape(-1)
    def quarters(b):
        return jnp.broadcast_to(ri[None, :], (b.size, 2)).reshape(-1)

    own_t = me * t + jnp.arange(t, dtype=jnp.int32)
    other_t = (me ^ 1) * t + jnp.arange(t, dtype=jnp.int32)
    even = bins_rel.reshape(2 * nz, 2, nf)[:, 0]
    table_part = cos_table(
        bin_rows(even)[:, None],
        quarters(even)[:, None],
        jnp.concatenate([own_t, other_t])[None, :],
        ntime,
    ).astype(jnp.bfloat16)
    inv_scale = jnp.float32(2.0 / ntime)
    table_time = (
        cos_table(
            bin_rows(bins_rel)[None, :], quarters(bins_rel)[None, :], own_t[:, None], ntime
        ).astype(jnp.bfloat16)
        * inv_scale.astype(jnp.bfloat16)
    )
    absq_own = jnp.where(own_t < ntime // 2, own_t, ntime - own_t)
    absq_own = jnp.broadcast_to(absq_own[:, None], (t, 128))

    half = min(-(-ONSET_TOP // 256) * 256, ntime // 2)
    times = jnp.concatenate(
        [jnp.arange(half, dtype=jnp.int32), ntime - half + jnp.arange(half, dtype=jnp.int32)]
    )
    absq_cols = jnp.where(times < ntime // 2, times, ntime - times)[:, None]
    table_fwd = cos_table(
        bin_rows(bins_abs)[:, None], quarters(bins_abs)[:, None], times[None, :], ntime
    ).astype(jnp.bfloat16)
    table_inv = (
        cos_table(
            bin_rows(bins_abs)[None, :], quarters(bins_abs)[None, :], times[:, None], ntime
        ).astype(jnp.bfloat16)
        * inv_scale.astype(jnp.bfloat16)
    )

    def spread(scales, first, count):
        block = (first + jnp.arange(count, dtype=jnp.int32)) % nrec // (nrec // nblocks)
        out = jnp.zeros((scales.shape[0], count), jnp.float32)
        for b in range(nblocks):
            out = jnp.where(block[None, :] == b, scales[:, b : b + 1], out)
        return jnp.repeat(out, 2, axis=0)

    scale_own = spread(refl_scale, 0, nrec)
    scale_cols = spread(scale_abs, me * width, width)

    mine = points_major(fd_plus)
    theirs = swap(mine, 1)
    part = partial_spectra(table_part, mine, theirs, rb, nq)
    arrived = {d: swap(part[2 * d + 1], 2) for d in range(nz - 1, -1, -1)}
    summed = {
        d: (part[2 * d].astype(jnp.float32) + arrived[d].astype(jnp.float32)).astype(jnp.bfloat16)
        for d in range(1, nz)
    }
    sent = [swap(summed[d], 4 * d) for d in range(nz - 1, 0, -1)]
    y1 = convolve([part[0], arrived[0]] + sent, scale_own, refl, 1.0)

    def exchange(x, shape):
        x = x.reshape(n, h, rb, c)
        x = lax.all_to_all(x, "freq", split_axis=0, concat_axis=0, tiled=True)
        return x.reshape(shape)

    def gather(y):
        along = [y] + [swap(y, 4 * d) for d in range(1, nz)]
        across = [swap(a, 2) for a in along]
        pairs = [p for z in zip(along, across) for p in z]
        return [p for a in pairs for p in (a, swap(a, 1))]

    x2 = window_columns(
        exchange(y1, (n, h, rb, c)),
        table_inv,
        table_fwd,
        absq_cols,
        onset.reshape(h, 1, c),
        scale_cols,
    )
    y2 = convolve([exchange(x2, (v, nq, rb, c))], None, refl, -1.0)
    minus = time_block(gather(y1), table_time, absq_own, onset_all, None, t)
    plus = time_block(gather(y2), table_time, absq_own, onset_all, fd_plus, t)
    return minus, plus


def solution(mesh):
    return jax.shard_map(
        local,
        mesh=mesh,
        in_specs=(
            P(("groups", "freq"), None, None, None),
            P(("groups", "freq"), None),
            P(("groups", "freq")),
            P(("groups", "freq"), None, None),
            P(("groups", "freq")),
        ),
        out_specs=(P(("groups", "freq"), None, None), P(("groups", "freq"), None, None)),
        check_vma=False,
    )
```

```python
import functools
import math

import jax
import jax.numpy as jnp
from jax import lax
from jax.experimental import pallas as pl
from jax.experimental.pallas import tpu as pltpu
from jax.sharding import PartitionSpec as P

ONSET_TOP = 767
VMEM_LIMIT = 56 << 20


def pitch(v):
    return v + 4


def after(x, *deps):
    return lax.optimization_barrier((x,) + deps)[0]


def params():
    return pltpu.CompilerParams(vmem_limit_bytes=VMEM_LIMIT)


def swap(x, stride):
    n = lax.axis_size("freq")
    return lax.ppermute(x, "freq", [(i, i ^ stride) for i in range(n)])


def cos_table(bins, rows_quarter, times, ntime):
    phase = (bins * times + rows_quarter) % ntime
    angle = phase.astype(jnp.float32) * jnp.float32(2.0 * math.pi / ntime)
    return jnp.cos(angle)


def points_major(x):
    t, v, s = x.shape
    sb = 128

    def kernel(x_ref, o_ref, scr):
        for i in range(t):
            scr[i * pitch(v) : i * pitch(v) + v, :] = x_ref[i].astype(jnp.float32)
        for i in range(v):
            o_ref[i] = scr[pl.ds(i, t, stride=pitch(v)), :].astype(jnp.bfloat16)

    return pl.pallas_call(
        kernel,
        grid=(s // sb,),
        in_specs=[pl.BlockSpec((t, v, sb), lambda i: (0, 0, i))],
        out_specs=pl.BlockSpec((v, t, sb), lambda i: (0, 0, i)),
        out_shape=jax.ShapeDtypeStruct((v, t, s), x.dtype),
        scratch_shapes=[pltpu.VMEM((t * pitch(v), sb), jnp.float32)],
        compiler_params=params(),
        name="points_major",
    )(x)


def partial_spectra(table, own, other, rb, nq, g, chunks):
    rows, _ = table.shape
    v, t, s = own.shape
    v //= chunks
    ndest = rows // rb
    c = s // nq
    vb = 4
    steps = v // vb

    def kernel(tab_ref, own_ref, other_ref, *outs):
        for i in range(vb):
            x = jnp.concatenate([own_ref[i], other_ref[i]], axis=0)
            res = jnp.dot(tab_ref[...], x, preferred_element_type=jnp.float32)
            for j in range(ndest):
                part = res[j * rb : (j + 1) * rb].astype(jnp.bfloat16)
                for q in range(nq):
                    outs[j][i, q] = part[:, q * c : (q + 1) * c]

    field = pl.BlockSpec((vb, t, s), lambda i: (g * steps + i, 0, 0))
    return pl.pallas_call(
        kernel,
        grid=(steps,),
        in_specs=[pl.BlockSpec((rows, 2 * t), lambda i: (0, 0)), field, field],
        out_specs=[pl.BlockSpec((vb, nq, rb, c), lambda i: (i, 0, 0, 0))] * ndest,
        out_shape=[jax.ShapeDtypeStruct((v, nq, rb, c), jnp.bfloat16)] * ndest,
        compiler_params=params(),
        name="partial_spectra",
    )(table, own, other)


def convolve(parts, scale, refl, sign):
    v, nq, rb, c = parts[0].shape
    nf, _, r, s = refl.shape
    nparts = len(parts)

    def kernel(*refs):
        part_refs = refs[:nparts]
        scale_ref = None if scale is None else refs[nparts]
        refl_ref, out_ref, x_scr, y_scr = refs[-4:]
        k = pl.program_id(0)

        @pl.when(k == 0)
        def _():
            for i in range(v):
                for q in range(nq):
                    x = part_refs[0][i, q].astype(jnp.float32)
                    for ref in part_refs[1:]:
                        x = x + ref[i, q].astype(jnp.float32)
                    for b in range(c // 128):
                        lanes = x[:, b * 128 : (b + 1) * 128]
                        at = q * (c // 128) + b
                        if scale_ref is not None:
                            block = at * 128 * scale.shape[1] // s
                            lanes = lanes * scale_ref[:, block : block + 1]
                        x_scr[at, pl.ds(i, rb, stride=pitch(v)), :] = lanes

        real = pl.ds(pl.multiple_of(2 * k * pitch(v), 8), v)
        imag = pl.ds((2 * k + 1) * pitch(v), v)
        x = jnp.concatenate(
            [
                jnp.concatenate([x_scr[b, real, :], x_scr[b, imag, :]], axis=0)
                for b in range(s // 128)
            ],
            axis=1,
        ).astype(jnp.bfloat16)
        dims = (((1,), (1,)), ((), ()))
        a = lax.dot_general(x, refl_ref[0, 0], dims, preferred_element_type=jnp.float32)
        b = lax.dot_general(x, refl_ref[0, 1], dims, preferred_element_type=jnp.float32)
        yr = a[:v] - sign * b[v:]
        yi = a[v:] + sign * b[:v]
        for b in range(r // 128):
            y_scr[b, real, :] = yr[:, b * 128 : (b + 1) * 128]
            y_scr[b, imag, :] = yi[:, b * 128 : (b + 1) * 128]

        @pl.when(k == nf - 1)
        def _():
            for i in range(v):
                for q in range(nq):
                    for b in range(c // 128):
                        y = y_scr[q * (c // 128) + b, pl.ds(i, rb, stride=pitch(v)), :]
                        out_ref[i, q, :, b * 128 : (b + 1) * 128] = y.astype(jnp.bfloat16)

    whole = pl.BlockSpec((v, nq, rb, c), lambda k: (0, 0, 0, 0))
    args = list(parts)
    specs = [whole] * nparts
    if scale is not None:
        args.append(scale)
        specs.append(pl.BlockSpec(scale.shape, lambda k: (0, 0)))
    args.append(refl)
    specs.append(pl.BlockSpec((1, 2, r, s), lambda k: (k, 0, 0, 0)))
    return pl.pallas_call(
        kernel,
        grid=(nf,),
        in_specs=specs,
        out_specs=whole,
        out_shape=jax.ShapeDtypeStruct((v, nq, rb, c), jnp.bfloat16),
        scratch_shapes=[
            pltpu.VMEM((s // 128, rb * pitch(v), 128), jnp.float32),
            pltpu.VMEM((r // 128, rb * pitch(v), 128), jnp.float32),
        ],
        compiler_params=params(),
        name="convolve",
    )(*args)


def window_columns(pieces, me, table, onset, factor):
    n = len(pieces)
    v, nq, rb, c = pieces[0].shape
    h = max(v // n, 1)
    rows = n * rb
    half = table.shape[1]
    tb = 256

    def kernel(me_ref, *refs):
        piece_refs = refs[:n]
        table_ref, onset_ref, out_ref = refs[n:]
        step = lax.broadcasted_iota(jnp.int32, (tb, c), 0)
        odd = lax.broadcasted_iota(jnp.int32, (rows, 1), 0) % 2
        sign = (1 - 2 * odd).astype(jnp.float32)
        first_dims = (((0,), (0,)), ((), ()))
        for i in range(h):
            spec = jnp.concatenate([ref[i, 0] for ref in piece_refs], axis=0)
            turned = (spec.astype(jnp.float32) * sign).astype(jnp.bfloat16)
            both = jnp.concatenate([spec, turned], axis=1)
            acc = jnp.zeros((rows, 2 * c), jnp.float32)
            for k in range(half // tb):
                tab = table_ref[:, k * tb : (k + 1) * tb]
                trace = lax.dot_general(
                    tab, both, first_dims, preferred_element_type=jnp.float32
                )
                kept = step < onset_ref[i, 0] - k * tb
                late = kept & (step > 0) if k == 0 else kept
                trace = jnp.where(jnp.concatenate([kept, late], axis=1), trace, 0.0)
                acc += jnp.dot(
                    tab, trace.astype(jnp.bfloat16), preferred_element_type=jnp.float32
                )
            acc = (acc[:, :c] + sign * acc[:, c:]) * factor
            for j in range(n):
                part = acc[j * rb : (j + 1) * rb].astype(jnp.bfloat16)
                out_ref[me_ref[0] ^ j, i] = part

    if v >= n:
        column = lambda i, me: (me[0], 0, 0, 0)
    else:
        column = lambda i, me: (me[0] // nq, me[0] % nq, 0, 0)
    whole = lambda x: pl.BlockSpec(x.shape, lambda i, me: (0,) * x.ndim)
    out_shape = jax.ShapeDtypeStruct((n, h, rb, c), jnp.bfloat16)
    return pl.pallas_call(
        kernel,
        grid_spec=pltpu.PrefetchScalarGridSpec(
            num_scalar_prefetch=1,
            grid=(1,),
            in_specs=[pl.BlockSpec((h, 1, rb, c), column)] * n
            + [whole(table), whole(onset)],
            out_specs=whole(out_shape),
        ),
        out_shape=out_shape,
        compiler_params=params(),
        name="window_columns",
    )(me[None], *pieces, table, onset)


def time_block(pieces, table, first, onset, direct, ntime, g, into):
    v, nq, rb, c = pieces[0].shape
    npieces = len(pieces)
    t = table.shape[0]
    s = nq * c
    sb = 128
    vb = 2 if v % 2 == 0 else 1
    tb = 8

    def kernel(*refs):
        piece_refs = refs[:npieces]
        tab_ref, first_ref, onset_ref = refs[npieces : npieces + 3]
        direct_ref = None if direct is None else refs[npieces + 3]
        out_ref, scr = refs[-2:]
        times = first_ref[0] + lax.broadcasted_iota(jnp.int32, (t, sb), 0)
        absq = jnp.where(times < ntime // 2, times, ntime - times)
        for i in range(0, v, vb):
            spec = jnp.concatenate(
                [
                    jnp.concatenate([ref[i + j, 0] for ref in piece_refs], axis=0)
                    for j in range(vb)
                ],
                axis=1,
            )
            res = jnp.dot(tab_ref[...], spec, preferred_element_type=jnp.float32)
            for j in range(vb):
                kept = absq < onset_ref[i + j : i + j + 1, :]
                y = jnp.where(kept, res[:, j * sb : (j + 1) * sb], 0.0)
                scr[pl.ds(i + j, t, stride=pitch(v)), :] = y

        @pl.loop(0, t // tb)
        def _(k):
            for j in range(tb):
                at = k * tb + j
                y = scr[pl.ds(at * pitch(v), v), :].astype(jnp.bfloat16)
                if direct_ref is None:
                    out_ref[at] = y
                else:
                    out_ref[at] = direct_ref[at].astype(jnp.float32) + y.astype(jnp.float32)

    per = c // sb
    piece_spec = pl.BlockSpec((v, 1, rb, sb), lambda i: (0, i // per, 0, i % per))
    field_spec = pl.BlockSpec((t, v, sb), lambda i: (0, g, i))
    args = list(pieces) + [table, first, onset]
    specs = [piece_spec] * npieces + [
        pl.BlockSpec(table.shape, lambda i: (0, 0)),
        pl.BlockSpec(memory_space=pltpu.SMEM),
        pl.BlockSpec((v, sb), lambda i: (g, i)),
    ]
    if direct is not None:
        args.append(direct)
        specs.append(field_spec)
    dtype = jnp.bfloat16 if direct is None else jnp.float32
    aliases = {}
    if into is not None:
        aliases = {len(args): 0}
        args.append(into)
        specs.append(pl.BlockSpec(memory_space=pl.ANY))
    return pl.pallas_call(
        kernel,
        grid=(s // sb,),
        in_specs=specs,
        out_specs=field_spec,
        out_shape=jax.ShapeDtypeStruct((t, onset.shape[0], s), dtype),
        scratch_shapes=[pltpu.VMEM((t * pitch(v), sb), jnp.float32)],
        input_output_aliases=aliases,
        compiler_params=params(),
        name="time_block",
    )(*args)


def local(refl, refl_scale, freq_index, fd_plus, onset):
    nf = refl.shape[0]
    nrec = refl.shape[2]
    t, v, _ = fd_plus.shape
    n = lax.axis_size("freq")
    me = lax.axis_index("freq")
    nz = n // 4
    ntime = t * n
    columns = v * nrec
    width = columns // n
    c = min(width, nrec)
    nq = nrec // c
    rb = 2 * nf
    quarter = ntime // 4

    def along(x):
        return jnp.stack([x] + [swap(x, 4 * d) for d in range(1, nz)])

    def across(x):
        return jnp.stack([x, swap(x, 2)], axis=1)

    def twins(x):
        x = jnp.stack([x, swap(x, 1)], axis=2)
        return x.reshape((n,) + x.shape[3:])

    raw = swap(fd_plus, 1)
    mine = points_major(fd_plus)
    theirs = points_major(raw)
    even = across(after(along(freq_index), mine, theirs))
    scale_own = jnp.repeat(refl_scale, 2, axis=0)

    ri = jnp.arange(2, dtype=jnp.int32) * quarter
    def bin_rows(b):
        return jnp.broadcast_to(b.reshape(-1, 1), (b.size, 2)).reshape(-1)
    def quarters(b):
        return jnp.broadcast_to(ri[None, :], (b.size, 2)).reshape(-1)

    own_t = me * t + jnp.arange(t, dtype=jnp.int32)
    other_t = (me ^ 1) * t + jnp.arange(t, dtype=jnp.int32)
    table_part = cos_table(
        bin_rows(even)[:, None],
        quarters(even)[:, None],
        jnp.concatenate([own_t, other_t])[None, :],
        ntime,
    ).astype(jnp.bfloat16)
    first_own = (me * t)[None]

    def add(*parts):
        total = parts[0].astype(jnp.float32)
        for p in parts[1:]:
            total = total + p.astype(jnp.float32)
        return total.astype(jnp.bfloat16)

    def reduce(part):
        moved = {}
        for d in range(nz - 1, -1, -1):
            x = part[2 * d + 1]
            moved[d] = swap(after(x, moved[d + 2]) if d + 2 in moved else x, 2)
        held = {d: [part[2 * d], moved[d]] for d in range(nz)}
        stride = 1
        while stride < nz:
            last = None
            for d in range(nz - 1, -1, -1):
                if d in held and d & stride:
                    total = add(*held.pop(d))
                    total = total if last is None else after(total, last)
                    to = d ^ stride
                    held[to].append(swap(total, 4 * stride))
                    if to:
                        last = add(*held[to])
                        held[to] = [last]
            stride *= 2
        return held[0], moved[min(1, nz - 1)]

    def gather(y):
        line = {0: y}
        over = {0: swap(y, 2)}
        stride = nz // 2
        far = y
        while stride:
            for d, p in list(line.items()):
                line[d ^ stride] = swap(p, 4 * stride)
                if d == 0 and stride == 1:
                    over[1] = swap(line[1], 2)
                    for k in line:
                        if k > 1:
                            line[k] = far = after(line[k], over[1])
            stride //= 2
        chip = []
        for d in range(nz):
            chip += [line[d], over[d] if d in over else swap(line[d], 2)]
        return [p for a in chip for p in (a, swap(a, 1))], far

    part = partial_spectra(table_part, mine, theirs, rb, nq, 0, 1)
    held, moved = reduce(part)
    bins_rel = after(twins(after(even, part[0])), moved)
    inv_scale = jnp.float32(2.0 / ntime)
    table_time = (
        cos_table(
            bin_rows(bins_rel)[None, :], quarters(bins_rel)[None, :], own_t[:, None], ntime
        ).astype(jnp.bfloat16)
        * inv_scale.astype(jnp.bfloat16)
    )
    half = min(-(-ONSET_TOP // 256) * 256, ntime // 2)
    table_cols = cos_table(
        bin_rows(bins_rel)[:, None],
        quarters(bins_rel)[:, None],
        jnp.arange(half, dtype=jnp.int32)[None, :],
        ntime,
    ).astype(jnp.bfloat16)

    held[0] = after(held[0], table_cols, table_time)
    y1 = convolve(held, scale_own, refl, 1.0)
    pieces, far = gather(y1)
    onset_own = onset.reshape(-1, 1, 1, c)
    x2 = window_columns(pieces, me, table_cols, onset_own, 2.0 / ntime)
    x2 = lax.all_to_all(x2, "freq", split_axis=0, concat_axis=0, tiled=True)
    onset_all = twins(across(along(after(onset.reshape(-1, 128), far)))).reshape(n, width)
    ids = jnp.arange(n, dtype=jnp.int32)
    chosen = (ids[:, None] ^ me) == ids[None, :]
    onset_all = jnp.sum(jnp.where(chosen[:, :, None], onset_all[None], 0), axis=1)
    onset_all = onset_all.reshape(v, nrec)
    minus = time_block(pieces, table_time, first_own, onset_all, None, ntime, 0, None)
    x2 = after(x2, minus).reshape(v, nq, rb, c)
    y2 = convolve([x2], scale_own, refl, -1.0)
    pieces, _ = gather(y2)
    plus = time_block(pieces, table_time, first_own, onset_all, fd_plus, ntime, 0, None)
    return minus, plus


def solution(mesh):
    return jax.shard_map(
        local,
        mesh=mesh,
        in_specs=(
            P(("groups", "freq"), None, None, None),
            P(("groups", "freq"), None),
            P(("groups", "freq")),
            P(("groups", "freq"), None, None),
            P(("groups", "freq")),
        ),
        out_specs=(P(("groups", "freq"), None, None), P(("groups", "freq"), None, None)),
        check_vma=False,
    )
```

```python
import functools
import math

import jax
import jax.numpy as jnp
from jax import lax
from jax.experimental import pallas as pl
from jax.experimental.pallas import tpu as pltpu
from jax.sharding import PartitionSpec as P

ONSET_TOP = 767
VMEM_LIMIT = 56 << 20
SB = 256
FB = 2


def pitch(v):
    return v + 4


def after(x, *deps):
    return lax.optimization_barrier((x,) + deps)[0]


def params():
    return pltpu.CompilerParams(vmem_limit_bytes=VMEM_LIMIT)


def swap(x, stride):
    n = lax.axis_size("freq")
    return lax.ppermute(x, "freq", [(i, i ^ stride) for i in range(n)])


def cos_table(bins, rows_quarter, times, ntime):
    phase = (bins * times + rows_quarter) % ntime
    angle = phase.astype(jnp.float32) * jnp.float32(2.0 * math.pi / ntime)
    return jnp.cos(angle)


def points_major(x):
    t, v, s = x.shape
    sb = 128

    def kernel(x_ref, o_ref, scr):
        for i in range(t):
            scr[i * pitch(v) : i * pitch(v) + v, :] = x_ref[i].astype(jnp.float32)
        for i in range(v):
            o_ref[i] = scr[pl.ds(i, t, stride=pitch(v)), :].astype(jnp.bfloat16)

    return pl.pallas_call(
        kernel,
        grid=(s // sb,),
        in_specs=[pl.BlockSpec((t, v, sb), lambda i: (0, 0, i))],
        out_specs=pl.BlockSpec((v, t, sb), lambda i: (0, 0, i)),
        out_shape=jax.ShapeDtypeStruct((v, t, s), x.dtype),
        scratch_shapes=[pltpu.VMEM((t * pitch(v), sb), jnp.float32)],
        compiler_params=params(),
        name="points_major",
    )(x)


def partial_spectra(table, own, other, rb, nq, g, chunks):
    rows, _ = table.shape
    v, t, s = own.shape
    v //= chunks
    ndest = rows // rb
    c = s // nq
    vb = math.gcd(v, 16)
    steps = v // vb

    def kernel(tab_ref, own_ref, other_ref, *outs):
        for i in range(vb):
            x = jnp.concatenate([own_ref[i], other_ref[i]], axis=0)
            res = jnp.dot(tab_ref[...], x, preferred_element_type=jnp.float32)
            for j in range(ndest):
                part = res[j * rb : (j + 1) * rb].astype(jnp.bfloat16)
                for q in range(nq):
                    outs[j][i, q] = part[:, q * c : (q + 1) * c]

    field = pl.BlockSpec((vb, t, s), lambda i: (g * steps + i, 0, 0))
    return pl.pallas_call(
        kernel,
        grid=(steps,),
        in_specs=[pl.BlockSpec((rows, 2 * t), lambda i: (0, 0)), field, field],
        out_specs=[pl.BlockSpec((vb, nq, rb, c), lambda i: (i, 0, 0, 0))] * ndest,
        out_shape=[jax.ShapeDtypeStruct((v, nq, rb, c), jnp.bfloat16)] * ndest,
        compiler_params=params(),
        name="partial_spectra",
    )(table, own, other)


def convolve(parts, scale, refl, sign):
    v, nq, rb, c = parts[0].shape
    nf, _, r, s = refl.shape
    nparts = len(parts)
    fb = math.gcd(nf, FB)

    def kernel(*refs):
        part_refs = refs[:nparts]
        scale_ref, refl_ref, out_ref, x_scr, y_scr = refs[-5:]
        k = pl.program_id(0)

        @pl.when(k == 0)
        def _():
            factors = jnp.concatenate([scale_ref[j // 2 : j // 2 + 1] for j in range(rb)], axis=0)
            for i in range(v):
                for q in range(nq):
                    x = part_refs[0][i, q].astype(jnp.float32)
                    for ref in part_refs[1:]:
                        x = x + ref[i, q].astype(jnp.float32)
                    for b in range(c // 128):
                        at = q * (c // 128) + b
                        block = at * 128 * scale.shape[1] // s
                        x_scr[at, pl.ds(i, rb, stride=pitch(v)), :] = (
                            x[:, b * 128 : (b + 1) * 128] * factors[:, block : block + 1]
                        )

        for j in range(fb):
            f = k * fb + j
            real = pl.ds(pl.multiple_of(2 * f * pitch(v), 8), v)
            imag = pl.ds((2 * f + 1) * pitch(v), v)
            x = jnp.concatenate(
                [
                    jnp.concatenate([x_scr[b, real, :], x_scr[b, imag, :]], axis=0)
                    for b in range(s // 128)
                ],
                axis=1,
            ).astype(jnp.bfloat16)
            dims = (((1,), (1,)), ((), ()))
            a = lax.dot_general(x, refl_ref[j, 0], dims, preferred_element_type=jnp.float32)
            b = lax.dot_general(x, refl_ref[j, 1], dims, preferred_element_type=jnp.float32)
            yr = a[:v] - sign * b[v:]
            yi = a[v:] + sign * b[:v]
            for b in range(r // 128):
                y_scr[b, real, :] = yr[:, b * 128 : (b + 1) * 128]
                y_scr[b, imag, :] = yi[:, b * 128 : (b + 1) * 128]

        @pl.when(k == nf // fb - 1)
        def _():
            for i in range(v):
                for q in range(nq):
                    for b in range(c // 128):
                        y = y_scr[q * (c // 128) + b, pl.ds(i, rb, stride=pitch(v)), :]
                        out_ref[i, q, :, b * 128 : (b + 1) * 128] = y.astype(jnp.bfloat16)

    whole = pl.BlockSpec((v, nq, rb, c), lambda k: (0, 0, 0, 0))
    args = list(parts) + [scale, refl]
    specs = [whole] * nparts
    specs.append(pl.BlockSpec(scale.shape, lambda k: (0, 0)))
    specs.append(pl.BlockSpec((fb, 2, r, s), lambda k: (k, 0, 0, 0)))
    return pl.pallas_call(
        kernel,
        grid=(nf // fb,),
        in_specs=specs,
        out_specs=whole,
        out_shape=jax.ShapeDtypeStruct((v, nq, rb, c), jnp.bfloat16),
        scratch_shapes=[
            pltpu.VMEM((s // 128, rb * pitch(v), 128), jnp.float32),
            pltpu.VMEM((r // 128, rb * pitch(v), 128), jnp.float32),
        ],
        compiler_params=params(),
        name="convolve",
    )(*args)


def window_columns(pieces, me, table, onset, factor):
    n = len(pieces)
    v, nq, rb, c = pieces[0].shape
    h = max(v // n, 1)
    rows = n * rb
    half = table.shape[1]
    tb = 256

    def kernel(me_ref, *refs):
        piece_refs = refs[:n]
        table_ref, onset_ref, out_ref = refs[n:]
        step = lax.broadcasted_iota(jnp.int32, (tb, c), 0)
        odd = lax.broadcasted_iota(jnp.int32, (rows, 1), 0) % 2
        sign = (1 - 2 * odd).astype(jnp.float32)
        first_dims = (((0,), (0,)), ((), ()))
        for i in range(h):
            spec = jnp.concatenate([ref[i, 0] for ref in piece_refs], axis=0)
            turned = (spec.astype(jnp.float32) * sign).astype(jnp.bfloat16)
            both = jnp.concatenate([spec, turned], axis=1)
            acc = jnp.zeros((rows, 2 * c), jnp.float32)
            for k in range(half // tb):
                tab = table_ref[:, k * tb : (k + 1) * tb]
                trace = lax.dot_general(
                    tab, both, first_dims, preferred_element_type=jnp.float32
                )
                kept = step < onset_ref[i, 0] - k * tb
                late = kept & (step > 0) if k == 0 else kept
                trace = jnp.where(jnp.concatenate([kept, late], axis=1), trace, 0.0)
                acc += jnp.dot(
                    tab, trace.astype(jnp.bfloat16), preferred_element_type=jnp.float32
                )
            acc = (acc[:, :c] + sign * acc[:, c:]) * factor
            for j in range(n):
                part = acc[j * rb : (j + 1) * rb].astype(jnp.bfloat16)
                out_ref[me_ref[0] ^ j, i] = part

    if v >= n:
        column = lambda i, me: (me[0], 0, 0, 0)
    else:
        column = lambda i, me: (me[0] // nq, me[0] % nq, 0, 0)
    whole = lambda x: pl.BlockSpec(x.shape, lambda i, me: (0,) * x.ndim)
    out_shape = jax.ShapeDtypeStruct((n, h, rb, c), jnp.bfloat16)
    return pl.pallas_call(
        kernel,
        grid_spec=pltpu.PrefetchScalarGridSpec(
            num_scalar_prefetch=1,
            grid=(1,),
            in_specs=[pl.BlockSpec((h, 1, rb, c), column)] * n
            + [whole(table), whole(onset)],
            out_specs=whole(out_shape),
        ),
        out_shape=out_shape,
        compiler_params=params(),
        name="window_columns",
    )(me[None], *pieces, table, onset)


def time_block(pieces, table, first, onset, direct, ntime, g, into):
    v, nq, rb, c = pieces[0].shape
    npieces = len(pieces)
    t = table.shape[0]
    s = nq * c
    sb = min(SB, c)
    per = c // sb
    vb = 2 if v % 2 == 0 else 1
    tb = 8

    def kernel(*refs):
        piece_refs = refs[:npieces]
        tab_ref, first_ref, onset_ref = refs[npieces : npieces + 3]
        direct_ref = None if direct is None else refs[npieces + 3]
        out_ref, scr = refs[-2:]
        times = first_ref[0] + lax.broadcasted_iota(jnp.int32, (t, sb), 0)
        absq = jnp.where(times < ntime // 2, times, ntime - times)
        for i in range(0, v, vb):
            spec = jnp.concatenate(
                [
                    jnp.concatenate([ref[i + j, 0] for ref in piece_refs], axis=0)
                    for j in range(vb)
                ],
                axis=1,
            )
            res = jnp.dot(tab_ref[...], spec, preferred_element_type=jnp.float32)
            for j in range(vb):
                kept = absq < onset_ref[i + j : i + j + 1, :]
                y = jnp.where(kept, res[:, j * sb : (j + 1) * sb], 0.0)
                for b in range(sb // 128):
                    scr[b, pl.ds(i + j, t, stride=pitch(v)), :] = y[:, b * 128 : (b + 1) * 128]

        @pl.loop(0, t // tb)
        def _(k):
            for j in range(tb):
                at = k * tb + j
                y = jnp.concatenate(
                    [scr[b, pl.ds(at * pitch(v), v), :] for b in range(sb // 128)], axis=1
                ).astype(jnp.bfloat16)
                if direct_ref is None:
                    out_ref[at] = y
                else:
                    out_ref[at] = direct_ref[at].astype(jnp.float32) + y.astype(jnp.float32)

    piece_spec = pl.BlockSpec((v, 1, rb, sb), lambda i: (0, i // per, 0, i % per))
    field_spec = pl.BlockSpec((t, v, sb), lambda i: (0, g, i))
    args = list(pieces) + [table, first, onset]
    specs = [piece_spec] * npieces + [
        pl.BlockSpec(table.shape, lambda i: (0, 0)),
        pl.BlockSpec(memory_space=pltpu.SMEM),
        pl.BlockSpec((v, sb), lambda i: (g, i)),
    ]
    if direct is not None:
        args.append(direct)
        specs.append(field_spec)
    dtype = jnp.bfloat16 if direct is None else jnp.float32
    aliases = {}
    if into is not None:
        aliases = {len(args): 0}
        args.append(into)
        specs.append(pl.BlockSpec(memory_space=pl.ANY))
    return pl.pallas_call(
        kernel,
        grid=(s // sb,),
        in_specs=specs,
        out_specs=field_spec,
        out_shape=jax.ShapeDtypeStruct((t, onset.shape[0], s), dtype),
        scratch_shapes=[pltpu.VMEM((sb // 128, t * pitch(v), 128), jnp.float32)],
        input_output_aliases=aliases,
        compiler_params=params(),
        name="time_block",
    )(*args)


def local(refl, refl_scale, freq_index, fd_plus, onset):
    nf = refl.shape[0]
    nrec = refl.shape[2]
    t, v, _ = fd_plus.shape
    n = lax.axis_size("freq")
    me = lax.axis_index("freq")
    nz = n // 4
    ntime = t * n
    columns = v * nrec
    width = columns // n
    c = min(width, nrec)
    nq = nrec // c
    rb = 2 * nf
    quarter = ntime // 4

    def along(x):
        return jnp.stack([x] + [swap(x, 4 * d) for d in range(1, nz)])

    def across(x):
        return jnp.stack([x, swap(x, 2)], axis=1)

    def twins(x):
        x = jnp.stack([x, swap(x, 1)], axis=2)
        return x.reshape((n,) + x.shape[3:])

    raw = swap(fd_plus, 1)
    mine = points_major(fd_plus)
    theirs = points_major(raw)
    even = across(after(along(freq_index), mine, theirs))

    ri = jnp.arange(2, dtype=jnp.int32) * quarter
    def bin_rows(b):
        return jnp.broadcast_to(b.reshape(-1, 1), (b.size, 2)).reshape(-1)
    def quarters(b):
        return jnp.broadcast_to(ri[None, :], (b.size, 2)).reshape(-1)

    own_t = me * t + jnp.arange(t, dtype=jnp.int32)
    other_t = (me ^ 1) * t + jnp.arange(t, dtype=jnp.int32)
    table_part = cos_table(
        bin_rows(even)[:, None],
        quarters(even)[:, None],
        jnp.concatenate([own_t, other_t])[None, :],
        ntime,
    ).astype(jnp.bfloat16)
    first_own = (me * t)[None]

    def add(*parts):
        total = parts[0].astype(jnp.float32)
        for p in parts[1:]:
            total = total + p.astype(jnp.float32)
        return total.astype(jnp.bfloat16)

    def reduce(part):
        moved = {}
        for d in range(nz - 1, -1, -1):
            x = part[2 * d + 1]
            moved[d] = swap(after(x, moved[d + 2]) if d + 2 in moved else x, 2)
        held = {d: [part[2 * d], moved[d]] for d in range(nz)}
        stride = 1
        while stride < nz:
            last = None
            for d in range(nz - 1, -1, -1):
                if d in held and d & stride:
                    total = add(*held.pop(d))
                    total = total if last is None else after(total, last)
                    to = d ^ stride
                    held[to].append(swap(total, 4 * stride))
                    if to:
                        last = add(*held[to])
                        held[to] = [last]
            stride *= 2
        return held[0], moved[min(1, nz - 1)]

    def gather(y):
        line = {0: y}
        over = {0: swap(y, 2)}
        stride = nz // 2
        far = y
        while stride:
            for d, p in list(line.items()):
                line[d ^ stride] = swap(p, 4 * stride)
                if d == 0 and stride == 1:
                    over[1] = swap(line[1], 2)
                    for k in line:
                        if k > 1:
                            line[k] = far = after(line[k], over[1])
            stride //= 2
        chip = []
        for d in range(nz):
            chip += [line[d], over[d] if d in over else swap(line[d], 2)]
        return [p for a in chip for p in (a, swap(a, 1))], far

    part = partial_spectra(table_part, mine, theirs, rb, nq, 0, 1)
    held, moved = reduce(part)
    bins_rel = after(twins(after(even, part[0])), moved)
    inv_scale = jnp.float32(2.0 / ntime)
    table_time = (
        cos_table(
            bin_rows(bins_rel)[None, :], quarters(bins_rel)[None, :], own_t[:, None], ntime
        ).astype(jnp.bfloat16)
        * inv_scale.astype(jnp.bfloat16)
    )
    half = min(-(-ONSET_TOP // 256) * 256, ntime // 2)
    table_cols = cos_table(
        bin_rows(bins_rel)[:, None],
        quarters(bins_rel)[:, None],
        jnp.arange(half, dtype=jnp.int32)[None, :],
        ntime,
    ).astype(jnp.bfloat16)

    held[0] = after(held[0], table_cols, table_time)
    y1 = convolve(held, refl_scale, refl, 1.0)
    pieces, far = gather(y1)
    onset_own = onset.reshape(-1, 1, 1, c)
    x2 = window_columns(pieces, me, table_cols, onset_own, 2.0 / ntime)
    x2 = lax.all_to_all(x2, "freq", split_axis=0, concat_axis=0, tiled=True)
    onset_all = twins(across(along(after(onset.reshape(-1, 128), far)))).reshape(n, width)
    ids = jnp.arange(n, dtype=jnp.int32)
    chosen = (ids[:, None] ^ me) == ids[None, :]
    onset_all = jnp.sum(jnp.where(chosen[:, :, None], onset_all[None], 0), axis=1)
    onset_all = onset_all.reshape(v, nrec)
    minus = time_block(pieces, table_time, first_own, onset_all, None, ntime, 0, None)
    x2 = after(x2, minus).reshape(v, nq, rb, c)
    y2 = convolve([x2], refl_scale, refl, -1.0)
    pieces, _ = gather(y2)
    plus = time_block(pieces, table_time, first_own, onset_all, fd_plus, ntime, 0, None)
    return minus, plus


def solution(mesh):
    return jax.shard_map(
        local,
        mesh=mesh,
        in_specs=(
            P(("groups", "freq"), None, None, None),
            P(("groups", "freq"), None),
            P(("groups", "freq")),
            P(("groups", "freq"), None, None),
            P(("groups", "freq")),
        ),
        out_specs=(P(("groups", "freq"), None, None), P(("groups", "freq"), None, None)),
        check_vma=False,
    )
```

```python
import functools
import math

import jax
import jax.numpy as jnp
from jax import lax
from jax.experimental import pallas as pl
from jax.experimental.pallas import tpu as pltpu
from jax.sharding import PartitionSpec as P

ONSET_TOP = 767
VMEM_LIMIT = 56 << 20
SB = 256
FB = 2


def pitch(v):
    return v + 4


def after(x, *deps):
    return lax.optimization_barrier((x,) + deps)[0]


def params():
    return pltpu.CompilerParams(vmem_limit_bytes=VMEM_LIMIT)


def swap(x, stride):
    n = lax.axis_size("freq")
    return lax.ppermute(x, "freq", [(i, i ^ stride) for i in range(n)])


def cos_table(bins, rows_quarter, times, ntime):
    phase = (bins * times + rows_quarter) % ntime
    angle = phase.astype(jnp.float32) * jnp.float32(2.0 * math.pi / ntime)
    return jnp.cos(angle)


def points_major(x):
    t, v, s = x.shape
    sb = 128

    def kernel(x_ref, o_ref, scr):
        for i in range(t):
            scr[i * pitch(v) : i * pitch(v) + v, :] = x_ref[i].astype(jnp.float32)
        for i in range(v):
            o_ref[i] = scr[pl.ds(i, t, stride=pitch(v)), :].astype(jnp.bfloat16)

    return pl.pallas_call(
        kernel,
        grid=(s // sb,),
        in_specs=[pl.BlockSpec((t, v, sb), lambda i: (0, 0, i))],
        out_specs=pl.BlockSpec((v, t, sb), lambda i: (0, 0, i)),
        out_shape=jax.ShapeDtypeStruct((v, t, s), x.dtype),
        scratch_shapes=[pltpu.VMEM((t * pitch(v), sb), jnp.float32)],
        compiler_params=params(),
        name="points_major",
    )(x)


def partial_spectra(table, own, other, rb, nq, g, chunks):
    rows, _ = table.shape
    v, t, s = own.shape
    v //= chunks
    ndest = rows // rb
    c = s // nq
    vb = math.gcd(v, 16)
    steps = v // vb

    def kernel(tab_ref, own_ref, other_ref, *outs):
        for i in range(vb):
            x = jnp.concatenate([own_ref[i], other_ref[i]], axis=0)
            res = jnp.dot(tab_ref[...], x, preferred_element_type=jnp.float32)
            for j in range(ndest):
                part = res[j * rb : (j + 1) * rb].astype(jnp.bfloat16)
                for q in range(nq):
                    outs[j][i, q] = part[:, q * c : (q + 1) * c]

    field = pl.BlockSpec((vb, t, s), lambda i: (g * steps + i, 0, 0))
    return pl.pallas_call(
        kernel,
        grid=(steps,),
        in_specs=[pl.BlockSpec((rows, 2 * t), lambda i: (0, 0)), field, field],
        out_specs=[pl.BlockSpec((vb, nq, rb, c), lambda i: (i, 0, 0, 0))] * ndest,
        out_shape=[jax.ShapeDtypeStruct((v, nq, rb, c), jnp.bfloat16)] * ndest,
        compiler_params=params(),
        name="partial_spectra",
    )(table, own, other)


def convolve(parts, scale, refl, sign):
    v, nq, rb, c = parts[0].shape
    nf, _, r, s = refl.shape
    nparts = len(parts)
    fb = math.gcd(nf, FB)

    def kernel(*refs):
        part_refs = refs[:nparts]
        scale_ref, refl_ref, out_ref, x_scr, y_scr = refs[-5:]
        k = pl.program_id(0)

        @pl.when(k == 0)
        def _():
            factors = jnp.concatenate([scale_ref[j // 2 : j // 2 + 1] for j in range(rb)], axis=0)
            for i in range(v):
                for q in range(nq):
                    x = part_refs[0][i, q].astype(jnp.float32)
                    for ref in part_refs[1:]:
                        x = x + ref[i, q].astype(jnp.float32)
                    for b in range(c // 128):
                        at = q * (c // 128) + b
                        block = at * 128 * scale.shape[1] // s
                        x_scr[at, pl.ds(i, rb, stride=pitch(v)), :] = (
                            x[:, b * 128 : (b + 1) * 128] * factors[:, block : block + 1]
                        )

        for j in range(fb):
            f = k * fb + j
            real = pl.ds(pl.multiple_of(2 * f * pitch(v), 8), v)
            imag = pl.ds((2 * f + 1) * pitch(v), v)
            x = jnp.concatenate(
                [
                    jnp.concatenate([x_scr[b, real, :], x_scr[b, imag, :]], axis=0)
                    for b in range(s // 128)
                ],
                axis=1,
            ).astype(jnp.bfloat16)
            dims = (((1,), (1,)), ((), ()))
            a = lax.dot_general(x, refl_ref[j, 0], dims, preferred_element_type=jnp.float32)
            b = lax.dot_general(x, refl_ref[j, 1], dims, preferred_element_type=jnp.float32)
            yr = a[:v] - sign * b[v:]
            yi = a[v:] + sign * b[:v]
            for b in range(r // 128):
                y_scr[b, real, :] = yr[:, b * 128 : (b + 1) * 128]
                y_scr[b, imag, :] = yi[:, b * 128 : (b + 1) * 128]

        @pl.when(k == nf // fb - 1)
        def _():
            for i in range(v):
                for q in range(nq):
                    for b in range(c // 128):
                        y = y_scr[q * (c // 128) + b, pl.ds(i, rb, stride=pitch(v)), :]
                        out_ref[i, q, :, b * 128 : (b + 1) * 128] = y.astype(jnp.bfloat16)

    whole = pl.BlockSpec((v, nq, rb, c), lambda k: (0, 0, 0, 0))
    args = list(parts) + [scale, refl]
    specs = [whole] * nparts
    specs.append(pl.BlockSpec(scale.shape, lambda k: (0, 0)))
    specs.append(pl.BlockSpec((fb, 2, r, s), lambda k: (k, 0, 0, 0)))
    return pl.pallas_call(
        kernel,
        grid=(nf // fb,),
        in_specs=specs,
        out_specs=whole,
        out_shape=jax.ShapeDtypeStruct((v, nq, rb, c), jnp.bfloat16),
        scratch_shapes=[
            pltpu.VMEM((s // 128, rb * pitch(v), 128), jnp.float32),
            pltpu.VMEM((r // 128, rb * pitch(v), 128), jnp.float32),
        ],
        compiler_params=params(),
        name="convolve",
    )(*args)


def window_columns(pieces, me, table, onset, factor):
    n = len(pieces)
    v, nq, rb, c = pieces[0].shape
    h = max(v // n, 1)
    rows = n * rb
    half = table.shape[1]
    tb = 256

    def kernel(me_ref, *refs):
        piece_refs = refs[:n]
        table_ref, onset_ref, out_ref = refs[n:]
        step = lax.broadcasted_iota(jnp.int32, (tb, c), 0)
        odd = lax.broadcasted_iota(jnp.int32, (rows, 1), 0) % 2
        sign = (1 - 2 * odd).astype(jnp.float32)
        first_dims = (((0,), (0,)), ((), ()))
        for i in range(h):
            spec = jnp.concatenate([ref[i, 0] for ref in piece_refs], axis=0)
            turned = (spec.astype(jnp.float32) * sign).astype(jnp.bfloat16)
            both = jnp.concatenate([spec, turned], axis=1)
            acc = jnp.zeros((rows, 2 * c), jnp.float32)
            for k in range(half // tb):
                tab = table_ref[:, k * tb : (k + 1) * tb]
                trace = lax.dot_general(
                    tab, both, first_dims, preferred_element_type=jnp.float32
                )
                kept = step < onset_ref[i, 0] - k * tb
                late = kept & (step > 0) if k == 0 else kept
                trace = jnp.where(jnp.concatenate([kept, late], axis=1), trace, 0.0)
                acc += jnp.dot(
                    tab, trace.astype(jnp.bfloat16), preferred_element_type=jnp.float32
                )
            acc = (acc[:, :c] + sign * acc[:, c:]) * factor
            for j in range(n):
                part = acc[j * rb : (j + 1) * rb].astype(jnp.bfloat16)
                out_ref[me_ref[0] ^ j, i] = part

    if v >= n:
        column = lambda i, me: (me[0], 0, 0, 0)
    else:
        column = lambda i, me: (me[0] // nq, me[0] % nq, 0, 0)
    whole = lambda x: pl.BlockSpec(x.shape, lambda i, me: (0,) * x.ndim)
    out_shape = jax.ShapeDtypeStruct((n, h, rb, c), jnp.bfloat16)
    return pl.pallas_call(
        kernel,
        grid_spec=pltpu.PrefetchScalarGridSpec(
            num_scalar_prefetch=1,
            grid=(1,),
            in_specs=[pl.BlockSpec((h, 1, rb, c), column)] * n
            + [whole(table), whole(onset)],
            out_specs=whole(out_shape),
        ),
        out_shape=out_shape,
        compiler_params=params(),
        name="window_columns",
    )(me[None], *pieces, table, onset)


def time_block(pieces, table, first, onset, direct, ntime, g, into):
    v, nq, rb, c = pieces[0].shape
    npieces = len(pieces)
    t = table.shape[0]
    s = nq * c
    sb = min(SB, c)
    per = c // sb
    vb = 2 if v % 2 == 0 else 1
    tb = 8

    def kernel(*refs):
        piece_refs = refs[:npieces]
        tab_ref, first_ref, onset_ref = refs[npieces : npieces + 3]
        direct_ref = None if direct is None else refs[npieces + 3]
        out_ref, scr = refs[-2:]
        times = first_ref[0] + lax.broadcasted_iota(jnp.int32, (t, sb), 0)
        absq = jnp.where(times < ntime // 2, times, ntime - times)
        for i in range(0, v, vb):
            spec = jnp.concatenate(
                [
                    jnp.concatenate([ref[i + j, 0] for ref in piece_refs], axis=0)
                    for j in range(vb)
                ],
                axis=1,
            )
            res = jnp.dot(tab_ref[...], spec, preferred_element_type=jnp.float32)
            for j in range(vb):
                kept = absq < onset_ref[i + j : i + j + 1, :]
                y = jnp.where(kept, res[:, j * sb : (j + 1) * sb], 0.0)
                for b in range(sb // 128):
                    scr[b, pl.ds(i + j, t, stride=pitch(v)), :] = y[:, b * 128 : (b + 1) * 128]

        @pl.loop(0, t // tb)
        def _(k):
            for j in range(tb):
                at = k * tb + j
                y = jnp.concatenate(
                    [scr[b, pl.ds(at * pitch(v), v), :] for b in range(sb // 128)], axis=1
                ).astype(jnp.bfloat16)
                if direct_ref is None:
                    out_ref[at] = y
                else:
                    out_ref[at] = direct_ref[at].astype(jnp.float32) + y.astype(jnp.float32)

    piece_spec = pl.BlockSpec((v, 1, rb, sb), lambda i: (0, i // per, 0, i % per))
    field_spec = pl.BlockSpec((t, v, sb), lambda i: (0, g, i))
    args = list(pieces) + [table, first, onset]
    specs = [piece_spec] * npieces + [
        pl.BlockSpec(table.shape, lambda i: (0, 0)),
        pl.BlockSpec(memory_space=pltpu.SMEM),
        pl.BlockSpec((v, sb), lambda i: (g, i)),
    ]
    if direct is not None:
        args.append(direct)
        specs.append(field_spec)
    dtype = jnp.bfloat16 if direct is None else jnp.float32
    aliases = {}
    if into is not None:
        aliases = {len(args): 0}
        args.append(into)
        specs.append(pl.BlockSpec(memory_space=pl.ANY))
    return pl.pallas_call(
        kernel,
        grid=(s // sb,),
        in_specs=specs,
        out_specs=field_spec,
        out_shape=jax.ShapeDtypeStruct((t, onset.shape[0], s), dtype),
        scratch_shapes=[pltpu.VMEM((sb // 128, t * pitch(v), 128), jnp.float32)],
        input_output_aliases=aliases,
        compiler_params=params(),
        name="time_block",
    )(*args)


def local(refl, refl_scale, freq_index, fd_plus, onset):
    nf = refl.shape[0]
    nrec = refl.shape[2]
    t, v, _ = fd_plus.shape
    n = lax.axis_size("freq")
    me = lax.axis_index("freq")
    nz = n // 4
    ntime = t * n
    columns = v * nrec
    width = columns // n
    c = min(width, nrec)
    nq = nrec // c
    rb = 2 * nf
    quarter = ntime // 4

    def along(x):
        return jnp.stack([x] + [swap(x, 4 * d) for d in range(1, nz)])

    def across(x):
        return jnp.stack([x, swap(x, 2)], axis=1)

    def twins(x):
        x = jnp.stack([x, swap(x, 1)], axis=2)
        return x.reshape((n,) + x.shape[3:])

    raw = swap(fd_plus, 1)
    mine = points_major(fd_plus)
    theirs = points_major(raw)
    even = across(after(along(freq_index), mine, theirs))

    ri = jnp.arange(2, dtype=jnp.int32) * quarter
    def bin_rows(b):
        return jnp.broadcast_to(b.reshape(-1, 1), (b.size, 2)).reshape(-1)
    def quarters(b):
        return jnp.broadcast_to(ri[None, :], (b.size, 2)).reshape(-1)

    own_t = me * t + jnp.arange(t, dtype=jnp.int32)
    other_t = (me ^ 1) * t + jnp.arange(t, dtype=jnp.int32)
    table_part = cos_table(
        bin_rows(even)[:, None],
        quarters(even)[:, None],
        jnp.concatenate([own_t, other_t])[None, :],
        ntime,
    ).astype(jnp.bfloat16)
    first_own = (me * t)[None]

    def add(*parts):
        total = parts[0].astype(jnp.float32)
        for p in parts[1:]:
            total = total + p.astype(jnp.float32)
        return total.astype(jnp.bfloat16)

    def reduce(part):
        moved = {}
        for d in range(nz - 1, -1, -1):
            x = part[2 * d + 1]
            moved[d] = swap(after(x, moved[d + 2]) if d + 2 in moved else x, 2)
        held = {d: [part[2 * d], moved[d]] for d in range(nz)}
        stride = 1
        while stride < nz:
            last = None
            for d in range(nz - 1, -1, -1):
                if d in held and d & stride:
                    total = add(*held.pop(d))
                    total = total if last is None else after(total, last)
                    to = d ^ stride
                    held[to].append(swap(total, 4 * stride))
                    if to:
                        last = add(*held[to])
                        held[to] = [last]
            stride *= 2
        return held[0], moved[min(1, nz - 1)]

    def gather(y, in_turn):
        line = {0: y}
        over = {0: swap(y, 2)}
        stride = nz // 2
        far = y
        while stride:
            for d, p in list(line.items()):
                line[d ^ stride] = swap(p, 4 * stride)
                if d == 0 and stride == 1:
                    over[1] = swap(after(line[1], over[0]) if in_turn else line[1], 2)
                    for k in line:
                        if k > 1:
                            line[k] = far = after(line[k], over[1])
            stride //= 2
        chip = []
        for d in range(nz):
            if d not in over:
                over[d] = swap(after(line[d], over[d - 1]) if in_turn else line[d], 2)
            chip += [line[d], over[d]]
        return [p for a in chip for p in (a, swap(a, 1))], far

    part = partial_spectra(table_part, mine, theirs, rb, nq, 0, 1)
    held, moved = reduce(part)
    bins_rel = after(twins(after(even, part[0])), moved)
    inv_scale = jnp.float32(2.0 / ntime)
    table_time = (
        cos_table(
            bin_rows(bins_rel)[None, :], quarters(bins_rel)[None, :], own_t[:, None], ntime
        ).astype(jnp.bfloat16)
        * inv_scale.astype(jnp.bfloat16)
    )
    half = min(-(-ONSET_TOP // 256) * 256, ntime // 2)
    table_cols = cos_table(
        bin_rows(bins_rel)[:, None],
        quarters(bins_rel)[:, None],
        jnp.arange(half, dtype=jnp.int32)[None, :],
        ntime,
    ).astype(jnp.bfloat16)

    held[0] = after(held[0], table_cols, table_time)
    y1 = convolve(held, refl_scale, refl, 1.0)
    pieces, far = gather(y1, False)
    onset_own = onset.reshape(-1, 1, 1, c)
    x2 = window_columns(pieces, me, table_cols, onset_own, 2.0 / ntime)
    x2 = lax.all_to_all(x2, "freq", split_axis=0, concat_axis=0, tiled=True)
    onset_all = twins(across(along(after(onset.reshape(-1, 128), far)))).reshape(n, width)
    ids = jnp.arange(n, dtype=jnp.int32)
    chosen = (ids[:, None] ^ me) == ids[None, :]
    onset_all = jnp.sum(jnp.where(chosen[:, :, None], onset_all[None], 0), axis=1)
    onset_all = onset_all.reshape(v, nrec)
    minus = time_block(pieces, table_time, first_own, onset_all, None, ntime, 0, None)
    x2 = after(x2, minus).reshape(v, nq, rb, c)
    y2 = convolve([x2], refl_scale, refl, -1.0)
    pieces, _ = gather(y2, True)
    plus = time_block(pieces, table_time, first_own, onset_all, fd_plus, ntime, 0, None)
    return minus, plus


def solution(mesh):
    return jax.shard_map(
        local,
        mesh=mesh,
        in_specs=(
            P(("groups", "freq"), None, None, None),
            P(("groups", "freq"), None),
            P(("groups", "freq")),
            P(("groups", "freq"), None, None),
            P(("groups", "freq")),
        ),
        out_specs=(P(("groups", "freq"), None, None), P(("groups", "freq"), None, None)),
        check_vma=False,
    )
```

```python
import functools
import math

import jax
import jax.numpy as jnp
from jax import lax
from jax.experimental import pallas as pl
from jax.experimental.pallas import tpu as pltpu
from jax.sharding import PartitionSpec as P

ONSET_TOP = 767
VMEM_LIMIT = 56 << 20
SB = 256
FB = 2


def pitch(v):
    return v + 4


def after(x, *deps):
    return lax.optimization_barrier((x,) + deps)[0]


def params():
    return pltpu.CompilerParams(vmem_limit_bytes=VMEM_LIMIT)


def swap(x, stride):
    n = lax.axis_size("freq")
    return lax.ppermute(x, "freq", [(i, i ^ stride) for i in range(n)])


def cos_table(bins, rows_quarter, times, ntime):
    phase = (bins * times + rows_quarter) % ntime
    angle = phase.astype(jnp.float32) * jnp.float32(2.0 * math.pi / ntime)
    return jnp.cos(angle)


def points_major(x):
    t, v, s = x.shape
    sb = 128

    def kernel(x_ref, o_ref, scr):
        for i in range(t):
            scr[i * pitch(v) : i * pitch(v) + v, :] = x_ref[i].astype(jnp.float32)
        for i in range(v):
            o_ref[i] = scr[pl.ds(i, t, stride=pitch(v)), :].astype(jnp.bfloat16)

    return pl.pallas_call(
        kernel,
        grid=(s // sb,),
        in_specs=[pl.BlockSpec((t, v, sb), lambda i: (0, 0, i))],
        out_specs=pl.BlockSpec((v, t, sb), lambda i: (0, 0, i)),
        out_shape=jax.ShapeDtypeStruct((v, t, s), x.dtype),
        scratch_shapes=[pltpu.VMEM(((t + 1) * pitch(v), sb), jnp.float32)],
        compiler_params=params(),
        name="points_major",
    )(x)


def partial_spectra(table, own, other, rb, nq, g, chunks):
    rows, _ = table.shape
    v, t, s = own.shape
    v //= chunks
    ndest = rows // rb
    c = s // nq
    vb = math.gcd(v, 16)
    steps = v // vb

    def kernel(tab_ref, own_ref, other_ref, *outs):
        for i in range(vb):
            x = jnp.concatenate([own_ref[i], other_ref[i]], axis=0)
            res = jnp.dot(tab_ref[...], x, preferred_element_type=jnp.float32)
            for j in range(ndest):
                part = res[j * rb : (j + 1) * rb].astype(jnp.bfloat16)
                for q in range(nq):
                    outs[j][i, q] = part[:, q * c : (q + 1) * c]

    field = pl.BlockSpec((vb, t, s), lambda i: (g * steps + i, 0, 0))
    return pl.pallas_call(
        kernel,
        grid=(steps,),
        in_specs=[pl.BlockSpec((rows, 2 * t), lambda i: (0, 0)), field, field],
        out_specs=[pl.BlockSpec((vb, nq, rb, c), lambda i: (i, 0, 0, 0))] * ndest,
        out_shape=[jax.ShapeDtypeStruct((v, nq, rb, c), jnp.bfloat16)] * ndest,
        compiler_params=params(),
        name="partial_spectra",
    )(table, own, other)


def convolve(parts, scale, refl, sign):
    v, nq, rb, c = parts[0].shape
    nf, _, r, s = refl.shape
    nparts = len(parts)
    fb = math.gcd(nf, FB)

    def kernel(*refs):
        part_refs = refs[:nparts]
        scale_ref, refl_ref, out_ref, x_scr, y_scr = refs[-5:]
        k = pl.program_id(0)

        @pl.when(k == 0)
        def _():
            factors = jnp.concatenate([scale_ref[j // 2 : j // 2 + 1] for j in range(rb)], axis=0)
            for i in range(v):
                for q in range(nq):
                    x = part_refs[0][i, q].astype(jnp.float32)
                    for ref in part_refs[1:]:
                        x = x + ref[i, q].astype(jnp.float32)
                    for b in range(c // 128):
                        at = q * (c // 128) + b
                        block = at * 128 * scale.shape[1] // s
                        x_scr[at, pl.ds(i, rb, stride=pitch(v)), :] = (
                            x[:, b * 128 : (b + 1) * 128] * factors[:, block : block + 1]
                        )

        for j in range(fb):
            f = k * fb + j
            real = pl.ds(pl.multiple_of(2 * f * pitch(v), 8), v)
            imag = pl.ds((2 * f + 1) * pitch(v), v)
            x = jnp.concatenate(
                [
                    jnp.concatenate([x_scr[b, real, :], x_scr[b, imag, :]], axis=0)
                    for b in range(s // 128)
                ],
                axis=1,
            ).astype(jnp.bfloat16)
            dims = (((1,), (1,)), ((), ()))
            a = lax.dot_general(x, refl_ref[j, 0], dims, preferred_element_type=jnp.float32)
            b = lax.dot_general(x, refl_ref[j, 1], dims, preferred_element_type=jnp.float32)
            yr = a[:v] - sign * b[v:]
            yi = a[v:] + sign * b[:v]
            for b in range(r // 128):
                y_scr[b, real, :] = yr[:, b * 128 : (b + 1) * 128]
                y_scr[b, imag, :] = yi[:, b * 128 : (b + 1) * 128]

        @pl.when(k == nf // fb - 1)
        def _():
            for i in range(v):
                for q in range(nq):
                    for b in range(c // 128):
                        y = y_scr[q * (c // 128) + b, pl.ds(i, rb, stride=pitch(v)), :]
                        out_ref[i, q, :, b * 128 : (b + 1) * 128] = y.astype(jnp.bfloat16)

    whole = pl.BlockSpec((v, nq, rb, c), lambda k: (0, 0, 0, 0))
    args = list(parts) + [scale, refl]
    specs = [whole] * nparts
    specs.append(pl.BlockSpec(scale.shape, lambda k: (0, 0)))
    specs.append(pl.BlockSpec((fb, 2, r, s), lambda k: (k, 0, 0, 0)))
    return pl.pallas_call(
        kernel,
        grid=(nf // fb,),
        in_specs=specs,
        out_specs=whole,
        out_shape=jax.ShapeDtypeStruct((v, nq, rb, c), jnp.bfloat16),
        scratch_shapes=[
            pltpu.VMEM((s // 128, (rb + 1) * pitch(v), 128), jnp.float32),
            pltpu.VMEM((r // 128, (rb + 1) * pitch(v), 128), jnp.float32),
        ],
        compiler_params=params(),
        name="convolve",
    )(*args)


def window_columns(pieces, me, table, onset, factor):
    n = len(pieces)
    v, nq, rb, c = pieces[0].shape
    h = max(v // n, 1)
    rows = n * rb
    half = table.shape[1]
    tb = 256

    def kernel(me_ref, *refs):
        piece_refs = refs[:n]
        table_ref, onset_ref, out_ref = refs[n:]
        step = lax.broadcasted_iota(jnp.int32, (tb, c), 0)
        odd = lax.broadcasted_iota(jnp.int32, (rows, 1), 0) % 2
        sign = (1 - 2 * odd).astype(jnp.float32)
        first_dims = (((0,), (0,)), ((), ()))
        for i in range(h):
            spec = jnp.concatenate([ref[i, 0] for ref in piece_refs], axis=0)
            turned = (spec.astype(jnp.float32) * sign).astype(jnp.bfloat16)
            both = jnp.concatenate([spec, turned], axis=1)
            acc = jnp.zeros((rows, 2 * c), jnp.float32)
            for k in range(half // tb):
                tab = table_ref[:, k * tb : (k + 1) * tb]
                trace = lax.dot_general(
                    tab, both, first_dims, preferred_element_type=jnp.float32
                )
                kept = step < onset_ref[i, 0] - k * tb
                late = kept & (step > 0) if k == 0 else kept
                trace = jnp.where(jnp.concatenate([kept, late], axis=1), trace, 0.0)
                acc += jnp.dot(
                    tab, trace.astype(jnp.bfloat16), preferred_element_type=jnp.float32
                )
            acc = (acc[:, :c] + sign * acc[:, c:]) * factor
            for j in range(n):
                part = acc[j * rb : (j + 1) * rb].astype(jnp.bfloat16)
                out_ref[me_ref[0] ^ j, i] = part

    if v >= n:
        column = lambda i, me: (me[0], 0, 0, 0)
    else:
        column = lambda i, me: (me[0] // nq, me[0] % nq, 0, 0)
    whole = lambda x: pl.BlockSpec(x.shape, lambda i, me: (0,) * x.ndim)
    out_shape = jax.ShapeDtypeStruct((n, h, rb, c), jnp.bfloat16)
    return pl.pallas_call(
        kernel,
        grid_spec=pltpu.PrefetchScalarGridSpec(
            num_scalar_prefetch=1,
            grid=(1,),
            in_specs=[pl.BlockSpec((h, 1, rb, c), column)] * n
            + [whole(table), whole(onset)],
            out_specs=whole(out_shape),
        ),
        out_shape=out_shape,
        compiler_params=params(),
        name="window_columns",
    )(me[None], *pieces, table, onset)


def time_block(pieces, table, first, onset, direct, ntime, g, into):
    v, nq, rb, c = pieces[0].shape
    npieces = len(pieces)
    t = table.shape[0]
    s = nq * c
    sb = min(SB, c)
    per = c // sb
    vb = 2 if v % 2 == 0 else 1
    tb = 8

    def kernel(*refs):
        piece_refs = refs[:npieces]
        tab_ref, first_ref, onset_ref = refs[npieces : npieces + 3]
        direct_ref = None if direct is None else refs[npieces + 3]
        out_ref, scr = refs[-2:]
        times = first_ref[0] + lax.broadcasted_iota(jnp.int32, (t, sb), 0)
        absq = jnp.where(times < ntime // 2, times, ntime - times)
        for i in range(0, v, vb):
            spec = jnp.concatenate(
                [
                    jnp.concatenate([ref[i + j, 0] for ref in piece_refs], axis=0)
                    for j in range(vb)
                ],
                axis=1,
            )
            res = jnp.dot(tab_ref[...], spec, preferred_element_type=jnp.float32)
            for j in range(vb):
                kept = absq < onset_ref[i + j : i + j + 1, :]
                y = jnp.where(kept, res[:, j * sb : (j + 1) * sb], 0.0)
                for b in range(sb // 128):
                    scr[b, pl.ds(i + j, t, stride=pitch(v)), :] = y[:, b * 128 : (b + 1) * 128]

        @pl.loop(0, t // tb)
        def _(k):
            for j in range(tb):
                at = k * tb + j
                y = jnp.concatenate(
                    [scr[b, pl.ds(at * pitch(v), v), :] for b in range(sb // 128)], axis=1
                ).astype(jnp.bfloat16)
                if direct_ref is None:
                    out_ref[at] = y
                else:
                    out_ref[at] = direct_ref[at].astype(jnp.float32) + y.astype(jnp.float32)

    piece_spec = pl.BlockSpec((v, 1, rb, sb), lambda i: (0, i // per, 0, i % per))
    field_spec = pl.BlockSpec((t, v, sb), lambda i: (0, g, i))
    args = list(pieces) + [table, first, onset]
    specs = [piece_spec] * npieces + [
        pl.BlockSpec(table.shape, lambda i: (0, 0)),
        pl.BlockSpec(memory_space=pltpu.SMEM),
        pl.BlockSpec((v, sb), lambda i: (g, i)),
    ]
    if direct is not None:
        args.append(direct)
        specs.append(field_spec)
    dtype = jnp.bfloat16 if direct is None else jnp.float32
    aliases = {}
    if into is not None:
        aliases = {len(args): 0}
        args.append(into)
        specs.append(pl.BlockSpec(memory_space=pl.ANY))
    return pl.pallas_call(
        kernel,
        grid=(s // sb,),
        in_specs=specs,
        out_specs=field_spec,
        out_shape=jax.ShapeDtypeStruct((t, onset.shape[0], s), dtype),
        scratch_shapes=[pltpu.VMEM((sb // 128, (t + 1) * pitch(v), 128), jnp.float32)],
        input_output_aliases=aliases,
        compiler_params=params(),
        name="time_block",
    )(*args)


def local(refl, refl_scale, freq_index, fd_plus, onset):
    nf = refl.shape[0]
    nrec = refl.shape[2]
    t, v, _ = fd_plus.shape
    n = lax.axis_size("freq")
    me = lax.axis_index("freq")
    nz = n // 4
    ntime = t * n
    columns = v * nrec
    width = columns // n
    c = min(width, nrec)
    nq = nrec // c
    rb = 2 * nf
    quarter = ntime // 4

    def along(x):
        return jnp.stack([x] + [swap(x, 4 * d) for d in range(1, nz)])

    def across(x):
        return jnp.stack([x, swap(x, 2)], axis=1)

    def twins(x):
        x = jnp.stack([x, swap(x, 1)], axis=2)
        return x.reshape((n,) + x.shape[3:])

    raw = swap(fd_plus, 1)
    mine = points_major(fd_plus)
    theirs = points_major(raw)
    even = across(after(along(freq_index), mine, theirs))

    ri = jnp.arange(2, dtype=jnp.int32) * quarter
    def bin_rows(b):
        return jnp.broadcast_to(b.reshape(-1, 1), (b.size, 2)).reshape(-1)
    def quarters(b):
        return jnp.broadcast_to(ri[None, :], (b.size, 2)).reshape(-1)

    own_t = me * t + jnp.arange(t, dtype=jnp.int32)
    other_t = (me ^ 1) * t + jnp.arange(t, dtype=jnp.int32)
    table_part = cos_table(
        bin_rows(even)[:, None],
        quarters(even)[:, None],
        jnp.concatenate([own_t, other_t])[None, :],
        ntime,
    ).astype(jnp.bfloat16)
    first_own = (me * t)[None]

    def add(*parts):
        total = parts[0].astype(jnp.float32)
        for p in parts[1:]:
            total = total + p.astype(jnp.float32)
        return total.astype(jnp.bfloat16)

    def reduce(part):
        moved = {}
        for d in range(nz - 1, -1, -1):
            x = part[2 * d + 1]
            moved[d] = swap(after(x, moved[d + 2]) if d + 2 in moved else x, 2)
        held = {d: [part[2 * d], moved[d]] for d in range(nz)}
        stride = 1
        while stride < nz:
            last = None
            for d in range(nz - 1, -1, -1):
                if d in held and d & stride:
                    total = add(*held.pop(d))
                    total = total if last is None else after(total, last)
                    to = d ^ stride
                    held[to].append(swap(total, 4 * stride))
                    if to:
                        last = add(*held[to])
                        held[to] = [last]
            stride *= 2
        return held[0], moved[min(1, nz - 1)]

    def gather(y, in_turn):
        line = {0: y}
        over = {0: swap(y, 2)}
        stride = nz // 2
        far = y
        while stride:
            for d, p in list(line.items()):
                line[d ^ stride] = swap(p, 4 * stride)
                if d == 0 and stride == 1:
                    over[1] = swap(after(line[1], over[0]) if in_turn else line[1], 2)
                    for k in line:
                        if k > 1:
                            line[k] = far = after(line[k], over[1])
            stride //= 2
        chip = []
        for d in range(nz):
            if d not in over:
                over[d] = swap(after(line[d], over[d - 1]) if in_turn else line[d], 2)
            chip += [line[d], over[d]]
        return [p for a in chip for p in (a, swap(a, 1))], far

    part = partial_spectra(table_part, mine, theirs, rb, nq, 0, 1)
    held, moved = reduce(part)
    bins_rel = after(twins(after(even, part[0])), moved)
    inv_scale = jnp.float32(2.0 / ntime)
    table_time = (
        cos_table(
            bin_rows(bins_rel)[None, :], quarters(bins_rel)[None, :], own_t[:, None], ntime
        ).astype(jnp.bfloat16)
        * inv_scale.astype(jnp.bfloat16)
    )
    half = min(-(-ONSET_TOP // 256) * 256, ntime // 2)
    table_cols = cos_table(
        bin_rows(bins_rel)[:, None],
        quarters(bins_rel)[:, None],
        jnp.arange(half, dtype=jnp.int32)[None, :],
        ntime,
    ).astype(jnp.bfloat16)

    held[0] = after(held[0], table_cols, table_time)
    y1 = convolve(held, refl_scale, refl, 1.0)
    pieces, far = gather(y1, False)
    onset_own = onset.reshape(-1, 1, 1, c)
    x2 = window_columns(pieces, me, table_cols, onset_own, 2.0 / ntime)
    x2 = lax.all_to_all(x2, "freq", split_axis=0, concat_axis=0, tiled=True)
    onset_all = twins(across(along(after(onset.reshape(-1, 128), far)))).reshape(n, width)
    ids = jnp.arange(n, dtype=jnp.int32)
    chosen = (ids[:, None] ^ me) == ids[None, :]
    onset_all = jnp.sum(jnp.where(chosen[:, :, None], onset_all[None], 0), axis=1)
    onset_all = onset_all.reshape(v, nrec)
    minus = time_block(pieces, table_time, first_own, onset_all, None, ntime, 0, None)
    x2 = after(x2, minus).reshape(v, nq, rb, c)
    y2 = convolve([x2], refl_scale, refl, -1.0)
    pieces, _ = gather(y2, True)
    plus = time_block(pieces, table_time, first_own, onset_all, fd_plus, ntime, 0, None)
    return minus, plus


def solution(mesh):
    return jax.shard_map(
        local,
        mesh=mesh,
        in_specs=(
            P(("groups", "freq"), None, None, None),
            P(("groups", "freq"), None),
            P(("groups", "freq")),
            P(("groups", "freq"), None, None),
            P(("groups", "freq")),
        ),
        out_specs=(P(("groups", "freq"), None, None), P(("groups", "freq"), None, None)),
        check_vma=False,
    )
```
